32 devices in a mesh: blk: 8 (over z, x), head: 4 (over y, core).
Axes of the slice: x: 2, y: 2, z: 4, core: 2. Of those that a mesh axis runs over, the one named last changes fastest.
Arguments:
- tokens: float32 [4096, 1536], P(('blk', 'head')), may hold values from -6 to 6
- cotangent: float32 [4096, 1536], P(('blk', 'head')), may hold values from -6 to 6
- doc_starts: int32 [4096], P('blk'), may hold values from 0 to 4095, as said below
- routes: int32 [4096, 6], P(('blk', 'head')), may hold values from 0 to 63, as said below
- expert_slots: int32 [4096, 6], P(('blk', 'head')), may hold values from -1 to 15, as said below
- norm_gains: float32 [2, 1536], P(None, ('blk', 'head')), may hold values from 0.25 to 1.75
- qkv_projection_weight: float32 [1536, 2560], P(('blk', 'head')), may hold values from -0.15625 to 0.15625
- w_out: float32 [1536, 1536], P(None, ('blk', 'head')), may hold values from -0.5 to 0.5
- w_router: float32 [1536, 64], P(('blk', 'head')), may hold values from -0.3125 to 0.3125
- w_moe_in: float32 [64, 1536, 1024], P('blk', 'head'), may hold values from -0.15625 to 0.15625
- w_moe_out: float32 [64, 512, 1536], P('blk', None, 'head'), may hold values from -0.5 to 0.5
- w_shared_in: float32 [1536, 2048], P(('blk', 'head')), may hold values from -0.15625 to 0.15625
- w_shared_out: float32 [1024, 1536], P(None, ('blk', 'head')), may hold values from -0.375 to 0.375
- mom_norm_gains: float32 [2, 1536], P(None, ('blk', 'head')), may hold values from -115.2 to 115.2
- momentum_qkv_weight: float32 [1536, 2560], P(('blk', 'head')), may hold values from -76.8 to 76.8
- mom_w_out: float32 [1536, 1536], P(None, ('blk', 'head')), may hold values from -115.2 to 115.2
- mom_w_router: float32 [1536, 64], P(('blk', 'head')), may hold values from -1152 to 1152
- mom_w_moe_in: float32 [64, 1536, 1024], P('blk', 'head'), may hold values from -24 to 24
- mom_w_moe_out: float32 [64, 512, 1536], P('blk', None, 'head'), may hold values from -24 to 24
- mom_w_shared_in: float32 [1536, 2048], P(('blk', 'head')), may hold values from -115.2 to 115.2
- mom_w_shared_out: float32 [1024, 1536], P(None, ('blk', 'head')), may hold values from -192 to 192
- avg_norm_gains: float32 [2, 1536], P(None, ('blk', 'head')), may hold values from 0.25 to 1.75
- averaged_qkv_weight: float32 [1536, 2560], P(('blk', 'head')), may hold values from -0.3125 to 0.3125
- avg_w_out: float32 [1536, 1536], P(None, ('blk', 'head')), may hold values from -0.5 to 0.5
- avg_w_router: float32 [1536, 64], P(('blk', 'head')), may hold values from -0.3125 to 0.3125
- avg_w_moe_in: float32 [64, 1536, 1024], P('blk', 'head'), may hold values from -0.3125 to 0.3125
- avg_w_moe_out: float32 [64, 512, 1536], P('blk', None, 'head'), may hold values from -0.5 to 0.5
- avg_w_shared_in: float32 [1536, 2048], P(('blk', 'head')), may hold values from -0.3125 to 0.3125
- avg_w_shared_out: float32 [1024, 1536], P(None, ('blk', 'head')), may hold values from -0.375 to 0.375
Outputs:
- output: float32 [4096, 1536], P(('blk', 'head'))
- grad_tokens: float32 [4096, 1536], P(('blk', 'head'))
- grad_norm_gains: float32 [2, 1536], P(None, ('blk', 'head'))
- new_norm_gains: float32 [2, 1536], P(None, ('blk', 'head'))
- next_mom_norm_gains: float32 [2, 1536], P(None, ('blk', 'head'))
- next_avg_norm_gains: float32 [2, 1536], P(None, ('blk', 'head'))
- grad_w_qkv: float32 [1536, 2560], P(('blk', 'head'))
- new_w_qkv: float32 [1536, 2560], P(('blk', 'head'))
- next_mom_w_qkv: float32 [1536, 2560], P(('blk', 'head'))
- next_avg_w_qkv: float32 [1536, 2560], P(('blk', 'head'))
- grad_w_out: float32 [1536, 1536], P(None, ('blk', 'head'))
- new_w_out: float32 [1536, 1536], P(None, ('blk', 'head'))
- next_mom_w_out: float32 [1536, 1536], P(None, ('blk', 'head'))
- next_avg_w_out: float32 [1536, 1536], P(None, ('blk', 'head'))
- grad_w_router: float32 [1536, 64], P(('blk', 'head'))
- new_w_router: float32 [1536, 64], P(('blk', 'head'))
- next_mom_w_router: float32 [1536, 64], P(('blk', 'head'))
- next_avg_w_router: float32 [1536, 64], P(('blk', 'head'))
- grad_w_moe_in: float32 [64, 1536, 1024], P('blk', 'head')
- new_w_moe_in: float32 [64, 1536, 1024], P('blk', 'head')
- next_mom_w_moe_in: float32 [64, 1536, 1024], P('blk', 'head')
- next_avg_w_moe_in: float32 [64, 1536, 1024], P('blk', 'head')
- grad_w_moe_out: float32 [64, 512, 1536], P('blk', None, 'head')
- step_w_moe_out: float32 [64, 512, 1536], P('blk', None, 'head')
- next_mom_w_moe_out: float32 [64, 512, 1536], P('blk', None, 'head')
- next_avg_w_moe_out: float32 [64, 512, 1536], P('blk', None, 'head')
- grad_w_shared_in: float32 [1536, 2048], P(('blk', 'head'))
- new_w_shared_in: float32 [1536, 2048], P(('blk', 'head'))
- next_mom_w_shared_in: float32 [1536, 2048], P(('blk', 'head'))
- next_avg_w_shared_in: float32 [1536, 2048], P(('blk', 'head'))
- grad_w_shared_out: float32 [1024, 1536], P(None, ('blk', 'head'))
- new_w_shared_out: float32 [1024, 1536], P(None, ('blk', 'head'))
- next_mom_w_shared_out: float32 [1024, 1536], P(None, ('blk', 'head'))
- next_avg_w_shared_out: float32 [1024, 1536], P(None, ('blk', 'head'))
The draws below stay inside these ranges and needn't reach their ends.
Inputs may be any that keep to these rules, and one draw needn't show every extreme that they name: `doc_starts`: never falling; each value is the position of its document's first token, at or before the token's own position; documents are at most 3072 long and one is exactly 3072 long; a multiple of 3072 starts a document unless it lies strictly inside a document of 3072 tokens. `routes`: each row names 6 different experts. `expert_slots`: within the 128 tokens of one device, the pairs that name one expert hold distinct cells 0 to 15; a pair holds -1 only when all 16 cells of its expert are taken by other pairs of that device; some expert's cells are all taken on every device.
All inputs are finite; a program needn't handle non-finite values.
Results may differ from the reference program's by a relative error of at most 0.025.
Values may be sent and summed in bfloat16 or wider, within the bound.
No kernel may reach another device: no remote copies, remote signals or barrier semaphores. Data moves between devices by JAX's collectives and lax.ppermute only.
A program may use at most 384 MiB of HBM per device.

```python
import jax
import jax.numpy as jnp
from jax import lax

MODEL_DIMENSION = 1536
QUERY_HEADS = 12
KEY_VALUE_HEADS = 4
HEAD_SIZE = 128
EXPERTS = 64
TOPK = 6
FE = 512
FS = 1024
TOK_DEV = 128
STREAM_TOKENS = 4096
DOC_MOST = 3072
CAP = 16


def route_table(key):
    base_key = jax.random.fold_in(key, 101)
    noise_key, order_key = jax.random.split(base_key)
    noise = jax.random.randint(noise_key, (STREAM_TOKENS, EXPERTS), 0, 1024)
    expert_order = jax.random.permutation(order_key, EXPERTS)
    expert_bias = jnp.where(expert_order == 0, 512, expert_order * 37 % 256)
    expert_ids = jnp.arange(EXPERTS, dtype=jnp.int32)
    score_codes = (noise + expert_bias[None, :]) * EXPERTS + expert_ids[None, :]
    top_codes, picked = lax.top_k(score_codes, TOPK)
    return picked.astype(jnp.int32)


def draw_routes(key, part):
    return route_table(key)


def draw_expert_slots(key, part):
    routes = route_table(key)
    block_count = STREAM_TOKENS // TOK_DEV
    pair_count = TOK_DEV * TOPK
    flat_routes = routes.reshape(block_count, pair_count)
    block_keys = jax.random.split(jax.random.fold_in(key, 202), block_count)
    priority = jax.vmap(lambda one_key: jax.random.permutation(one_key, pair_count))(block_keys).astype(jnp.int32)
    pair_codes = flat_routes * pair_count + priority
    pair_order = jnp.argsort(pair_codes, axis=1)
    sorted_expert = jnp.take_along_axis(flat_routes, pair_order, axis=1)
    expert_ids = jnp.arange(EXPERTS, dtype=jnp.int32)
    expert_counts = jnp.sum((flat_routes[:, :, None] == expert_ids[None, None, :]).astype(jnp.int32), axis=1)
    expert_firsts = jnp.cumsum(expert_counts, axis=1) - expert_counts
    sorted_ranks = jnp.arange(pair_count, dtype=jnp.int32)[None, :] - jnp.take_along_axis(expert_firsts, sorted_expert, axis=1)
    block_rows = jnp.arange(block_count, dtype=jnp.int32)[:, None]
    pair_ranks = jnp.zeros((block_count, pair_count), jnp.int32).at[block_rows, pair_order].set(sorted_ranks.astype(jnp.int32))
    slot_values = jnp.where(pair_ranks < CAP, pair_ranks, -1)
    return slot_values.reshape(STREAM_TOKENS, TOPK).astype(jnp.int32)


def draw_doc_starts(key, part):
    flag_key, start_key = jax.random.split(jax.random.fold_in(key, 303))
    position = jnp.arange(STREAM_TOKENS, dtype=jnp.int32)
    long_start = jax.random.randint(start_key, (), 0, STREAM_TOKENS - DOC_MOST + 1).astype(jnp.int32)
    long_end = long_start + DOC_MOST
    inside = (position > long_start) & (position < long_end)
    boundary = jax.random.randint(flag_key, (STREAM_TOKENS,), 0, STREAM_TOKENS) < 16
    boundary = boundary | (position % DOC_MOST == 0)
    boundary = jnp.where(inside, False, boundary)
    boundary = boundary | (position == 0) | (position == long_start) | (position == long_end)
    return lax.cummax(jnp.where(boundary, position, 0), axis=0).astype(jnp.int32)


def levels(own_key, extent, cuts, least, high):
    def one(axis_at, parts):
        steps = jax.random.uniform(jax.random.fold_in(jax.random.fold_in(own_key, 6), axis_at), (parts,), jnp.float32, least / len(cuts), high / len(cuts))
        return jnp.repeat(jnp.exp(steps), extent[axis_at] // parts).reshape((-1,) + (1,) * (len(extent) - axis_at - 1))

    level = one(*cuts[0])
    for cut in cuts[1:]:
        level = level * one(*cut)
    return level


def gaussian(rng, shape, scale, limit, pieces=(), held_as=jnp.bfloat16):
    array = jax.random.normal(rng, shape, jnp.float32) * scale
    if len(pieces) > 0:
        array = levels(rng, shape, pieces, -0.22, 0.18) * array
    return jnp.clip(array, min=-limit, max=limit).astype(held_as)


def setup_inputs(seed: int = 0) -> dict:
    splits = jax.random.split(jax.random.key(seed), 30)
    tokens = gaussian(splits[0], (STREAM_TOKENS, MODEL_DIMENSION), 1.0, 6.0, ((0, 32),), jnp.float32)
    cotangent = gaussian(splits[1], (STREAM_TOKENS, MODEL_DIMENSION), 1.0, 6.0, ((0, 32),), jnp.float32)
    doc_starts = draw_doc_starts(jax.random.fold_in(splits[29], 71), 0)
    routes = draw_routes(jax.random.fold_in(splits[29], 71), 0)
    expert_slots = draw_expert_slots(jax.random.fold_in(splits[29], 71), 0)
    norm_gains = jnp.clip(1.0 + 0.15 * jax.random.normal(splits[5], (2, MODEL_DIMENSION), jnp.float32), 0.25, 1.75)
    qkv_projection_weight = gaussian(splits[6], (MODEL_DIMENSION, (QUERY_HEADS + 2 * KEY_VALUE_HEADS) * HEAD_SIZE), MODEL_DIMENSION ** -0.5, 0.15625, ((0, 32),), jnp.float32)
    w_out = gaussian(splits[7], (QUERY_HEADS * HEAD_SIZE, MODEL_DIMENSION), HEAD_SIZE ** -0.5, 0.5, ((1, 32),), jnp.float32)
    w_router = gaussian(splits[8], (MODEL_DIMENSION, EXPERTS), (MODEL_DIMENSION // 4) ** -0.5, 0.3125, ((0, 32),), jnp.float32)
    w_moe_in = gaussian(splits[9], (EXPERTS, MODEL_DIMENSION, 2 * FE), MODEL_DIMENSION ** -0.5, 0.15625, ((0, 8), (1, 4)), jnp.float32)
    w_moe_out = gaussian(splits[10], (EXPERTS, FE, MODEL_DIMENSION), (FE // 4) ** -0.5, 0.5, ((0, 8), (2, 4)), jnp.float32)
    w_shared_in = gaussian(splits[11], (MODEL_DIMENSION, 2 * FS), MODEL_DIMENSION ** -0.5, 0.15625, ((0, 32),), jnp.float32)
    w_shared_out = gaussian(splits[12], (FS, MODEL_DIMENSION), (FS // 4) ** -0.5, 0.375, ((1, 32),), jnp.float32)
    mom_norm_gains = gaussian(splits[13], (2, MODEL_DIMENSION), (0.3 * STREAM_TOKENS ** 0.5), 115.2, ((1, 32),), jnp.float32)
    momentum_qkv_weight = gaussian(splits[14], (MODEL_DIMENSION, (QUERY_HEADS + 2 * KEY_VALUE_HEADS) * HEAD_SIZE), (0.2 * STREAM_TOKENS ** 0.5), 76.8, ((0, 32),), jnp.float32)
    mom_w_out = gaussian(splits[15], (QUERY_HEADS * HEAD_SIZE, MODEL_DIMENSION), (0.3 * STREAM_TOKENS ** 0.5), 115.2, ((1, 32),), jnp.float32)
    mom_w_router = gaussian(splits[16], (MODEL_DIMENSION, EXPERTS), (3.0 * STREAM_TOKENS ** 0.5), 1152.0, ((0, 32),), jnp.float32)
    mom_w_moe_in = gaussian(splits[17], (EXPERTS, MODEL_DIMENSION, 2 * FE), 4.0, 24.0, ((0, 8), (1, 4)), jnp.float32)
    mom_w_moe_out = gaussian(splits[18], (EXPERTS, FE, MODEL_DIMENSION), 4.0, 24.0, ((0, 8), (2, 4)), jnp.float32)
    mom_w_shared_in = gaussian(splits[19], (MODEL_DIMENSION, 2 * FS), (0.3 * STREAM_TOKENS ** 0.5), 115.2, ((0, 32),), jnp.float32)
    mom_w_shared_out = gaussian(splits[20], (FS, MODEL_DIMENSION), (0.5 * STREAM_TOKENS ** 0.5), 192.0, ((1, 32),), jnp.float32)
    avg_norm_gains = jnp.clip(1.0 + 0.15 * jax.random.normal(splits[21], (2, MODEL_DIMENSION), jnp.float32), 0.25, 1.75)
    averaged_qkv_weight = gaussian(splits[22], (MODEL_DIMENSION, (QUERY_HEADS + 2 * KEY_VALUE_HEADS) * HEAD_SIZE), (MODEL_DIMENSION // 4) ** -0.5, 0.3125, ((0, 32),), jnp.float32)
    avg_w_out = gaussian(splits[23], (QUERY_HEADS * HEAD_SIZE, MODEL_DIMENSION), HEAD_SIZE ** -0.5, 0.5, ((1, 32),), jnp.float32)
    avg_w_router = gaussian(splits[24], (MODEL_DIMENSION, EXPERTS), (MODEL_DIMENSION // 4) ** -0.5, 0.3125, ((0, 32),), jnp.float32)
    avg_w_moe_in = gaussian(splits[25], (EXPERTS, MODEL_DIMENSION, 2 * FE), (MODEL_DIMENSION // 4) ** -0.5, 0.3125, ((0, 8), (1, 4)), jnp.float32)
    avg_w_moe_out = gaussian(splits[26], (EXPERTS, FE, MODEL_DIMENSION), (FE // 4) ** -0.5, 0.5, ((0, 8), (2, 4)), jnp.float32)
    avg_w_shared_in = gaussian(splits[27], (MODEL_DIMENSION, 2 * FS), (MODEL_DIMENSION // 4) ** -0.5, 0.3125, ((0, 32),), jnp.float32)
    avg_w_shared_out = gaussian(splits[28], (FS, MODEL_DIMENSION), (FS // 4) ** -0.5, 0.375, ((1, 32),), jnp.float32)
    return {"tokens": tokens, "cotangent": cotangent, "doc_starts": doc_starts, "routes": routes, "expert_slots": expert_slots, "norm_gains": norm_gains, "qkv_projection_weight": qkv_projection_weight, "w_out": w_out, "w_router": w_router, "w_moe_in": w_moe_in, "w_moe_out": w_moe_out, "w_shared_in": w_shared_in, "w_shared_out": w_shared_out, "mom_norm_gains": mom_norm_gains, "momentum_qkv_weight": momentum_qkv_weight, "mom_w_out": mom_w_out, "mom_w_router": mom_w_router, "mom_w_moe_in": mom_w_moe_in, "mom_w_moe_out": mom_w_moe_out, "mom_w_shared_in": mom_w_shared_in, "mom_w_shared_out": mom_w_shared_out, "avg_norm_gains": avg_norm_gains, "averaged_qkv_weight": averaged_qkv_weight, "avg_w_out": avg_w_out, "avg_w_router": avg_w_router, "avg_w_moe_in": avg_w_moe_in, "avg_w_moe_out": avg_w_moe_out, "avg_w_shared_in": avg_w_shared_in, "avg_w_shared_out": avg_w_shared_out}


NORM_EPSILON = 1e-05
MASKED_SCORE = -1e+30
LEARN_RATE = 0.001
MOMENTUM = 0.5
DECAY = 0.5
FULL_PRECISION = lax.Precision.HIGHEST

@jax.custom_vjp
def low(v):
    return lax.optimization_barrier(v.astype(jnp.bfloat16)).astype(jnp.float32)

@jax.custom_vjp
def low_back(v):
    return v

def low_keep(v):
    return (low(v), None)

def low_pass(kept, grad):
    return (grad,)

def back_keep(v):
    return (v, None)

def back_low(kept, grad):
    return (low(grad),)
low.defvjp(low_keep, low_pass)
low_back.defvjp(back_keep, back_low)

def matmul(left_side, right_side):
    return jnp.dot(left_side, right_side, precision=FULL_PRECISION, preferred_element_type=jnp.float32)

def rms_norm(values, gain_row):
    return values * lax.rsqrt(lax.optimization_barrier(jnp.mean(values * values, axis=-1, keepdims=True)) + NORM_EPSILON) * gain_row

def attend(queries, key_rows, value_rows, doc_starts):
    token_count = queries.shape[0]
    block_rows = 512
    key_window = min(DOC_MOST + block_rows, token_count)
    score_scale = HEAD_SIZE ** (-0.5)

    def one_block(block_index):
        first_row = block_index * block_rows
        key_first = jnp.maximum(first_row + block_rows - key_window, 0).astype(jnp.int32)
        block_queries = lax.dynamic_slice_in_dim(queries, first_row, block_rows, 0)
        block_keys = lax.dynamic_slice_in_dim(key_rows, key_first, key_window, 0)
        block_values = lax.dynamic_slice_in_dim(value_rows, key_first, key_window, 0)
        block_starts = lax.dynamic_slice_in_dim(doc_starts, first_row, block_rows, 0)
        query_pos = first_row + jnp.arange(block_rows, dtype=jnp.int32)
        key_pos = key_first + jnp.arange(key_window, dtype=jnp.int32)
        visible = (key_pos[None, :] <= query_pos[:, None]) & (key_pos[None, :] >= block_starts[:, None])
        scores = low_back(jnp.einsum('qhrd,khd->qhrk', block_queries, block_keys, precision=FULL_PRECISION) * score_scale)
        scores = jnp.where(visible[:, None, None, :], scores, MASKED_SCORE)
        attention_weights = low(jax.nn.softmax(scores, axis=-1))
        return jnp.einsum('qhrk,khd->qhrd', attention_weights, block_values, precision=FULL_PRECISION)
    blocks = lax.map(jax.checkpoint(one_block), jnp.arange(token_count // block_rows, dtype=jnp.int32))
    return blocks.reshape(queries.shape)

def shared_branch(input_two, w_shared_in, w_shared_out):
    gate_up = low_back(matmul(input_two, w_shared_in))
    hidden = low(jax.nn.silu(gate_up[:, :FS]) * gate_up[:, FS:])
    return low_back(matmul(hidden, w_shared_out))

def expert_branch(input_two, router_logits, w_moe_in, w_moe_out, routes, expert_slots):
    device_count = STREAM_TOKENS // TOK_DEV
    cell_count = EXPERTS * CAP
    chosen = jnp.take_along_axis(router_logits, routes, axis=1)
    gate_probs = jax.nn.softmax(chosen, axis=-1)
    cell_codes = jnp.where(expert_slots >= 0, routes * CAP + expert_slots, -1)
    cell_index = jnp.arange(cell_count, dtype=jnp.int32)
    input_blocks = input_two.reshape(device_count, TOK_DEV, MODEL_DIMENSION)
    code_blocks = cell_codes.reshape(device_count, TOK_DEV, TOPK)
    gate_blocks = gate_probs.reshape(device_count, TOK_DEV, TOPK)

    def dispatch(block_args):
        input_block, code_block = block_args
        dispatch_table = jnp.any(code_block[:, :, None] == cell_index[None, None, :], axis=1).astype(jnp.float32)
        return jnp.einsum('tc,td->cd', dispatch_table, input_block, precision=FULL_PRECISION)
    buffers = low_back(lax.map(dispatch, (input_blocks, code_blocks)))
    buffers = buffers.reshape(device_count, EXPERTS, CAP, MODEL_DIMENSION).transpose(1, 0, 2, 3).reshape(EXPERTS, device_count * CAP, MODEL_DIMENSION)

    def expert(expert_args):
        rows_in, weight_in, weight_back = expert_args
        gate_up = low_back(matmul(rows_in, weight_in))
        hidden = low(jax.nn.silu(gate_up[:, :FE]) * gate_up[:, FE:])
        return low(low_back(matmul(hidden, weight_back)))
    expert_rows = lax.map(jax.checkpoint(expert), (buffers, w_moe_in, w_moe_out))
    expert_rows = expert_rows.reshape(EXPERTS, device_count, CAP, MODEL_DIMENSION).transpose(1, 0, 2, 3).reshape(device_count, cell_count, MODEL_DIMENSION)

    def combine(block_args):
        code_block, gate_block, row_block = block_args
        cell_match = code_block[:, :, None] == cell_index[None, None, :]
        combine_weights = low(lax.optimization_barrier(jnp.sum(jnp.where(cell_match, gate_block[:, :, None], 0.0), axis=1)))
        return matmul(combine_weights, row_block)
    combined = lax.map(combine, (code_blocks, gate_blocks, expert_rows))
    return low_back(combined.reshape(STREAM_TOKENS, MODEL_DIMENSION))

def forward(tokens, norm_gains, qkv_projection_weight, w_out, w_router, w_moe_in, w_moe_out, w_shared_in, w_shared_out, doc_starts, routes, expert_slots):
    heads_per_group = QUERY_HEADS // KEY_VALUE_HEADS
    gain_rows = low(norm_gains)
    input_one = low(rms_norm(tokens, gain_rows[0]))
    projected_rows = low(low_back(matmul(input_one, low(qkv_projection_weight))))
    projected_rows = projected_rows.reshape(STREAM_TOKENS, KEY_VALUE_HEADS, heads_per_group + 2, HEAD_SIZE)
    attn_rows = attend(projected_rows[:, :, :heads_per_group], projected_rows[:, :, heads_per_group], projected_rows[:, :, heads_per_group + 1], doc_starts)
    attn_rows = low(low_back(attn_rows)).reshape(STREAM_TOKENS, QUERY_HEADS * HEAD_SIZE)
    mixed_rows = tokens + low_back(matmul(attn_rows, low(w_out)))
    input_two = low(rms_norm(mixed_rows, gain_rows[1]))
    router_logits = low_back(matmul(input_two, low(w_router)))
    shared_rows = shared_branch(input_two, low(w_shared_in), low(w_shared_out))
    expert_out = expert_branch(input_two, router_logits, low(w_moe_in), low(w_moe_out), routes, expert_slots)
    return mixed_rows + shared_rows + expert_out

def apply_update(weight, gradient, moment, average):
    moment_new = MOMENTUM * moment + gradient
    change = -LEARN_RATE * (gradient + MOMENTUM * moment_new)
    weight_new = weight + change
    average_new = DECAY * average + (1.0 - DECAY) * weight_new
    return (weight_new, moment_new, average_new, change)

def reference(tokens, cotangent, doc_starts, routes, expert_slots, norm_gains, qkv_projection_weight, w_out, w_router, w_moe_in, w_moe_out, w_shared_in, w_shared_out, mom_norm_gains, momentum_qkv_weight, mom_w_out, mom_w_router, mom_w_moe_in, mom_w_moe_out, mom_w_shared_in, mom_w_shared_out, avg_norm_gains, averaged_qkv_weight, avg_w_out, avg_w_router, avg_w_moe_in, avg_w_moe_out, avg_w_shared_in, avg_w_shared_out):

    def layer_forward(token_arg, gain_arg, qkv_arg, out_arg, router_arg, moe_in_arg, moe_out_arg, shared_in_arg, shared_out_arg):
        return forward(token_arg, gain_arg, qkv_arg, out_arg, router_arg, moe_in_arg, moe_out_arg, shared_in_arg, shared_out_arg, doc_starts, routes, expert_slots)
    output, pullback = jax.vjp(layer_forward, tokens, norm_gains, qkv_projection_weight, w_out, w_router, w_moe_in, w_moe_out, w_shared_in, w_shared_out)
    grad_tokens, grad_norm_gains, grad_w_qkv, grad_w_out, grad_w_router, grad_w_moe_in, grad_w_moe_out, grad_w_shared_in, grad_w_shared_out = pullback(cotangent)
    new_norm_gains, next_mom_norm_gains, next_avg_norm_gains, unused_gains = apply_update(norm_gains, grad_norm_gains, mom_norm_gains, avg_norm_gains)
    new_w_qkv, next_mom_w_qkv, next_avg_w_qkv, unused_qkv = apply_update(qkv_projection_weight, grad_w_qkv, momentum_qkv_weight, averaged_qkv_weight)
    new_w_out, next_mom_w_out, next_avg_w_out, unused_out = apply_update(w_out, grad_w_out, mom_w_out, avg_w_out)
    new_w_router, next_mom_w_router, next_avg_w_router, unused_router = apply_update(w_router, grad_w_router, mom_w_router, avg_w_router)
    new_w_moe_in, next_mom_w_moe_in, next_avg_w_moe_in, unused_moe_in = apply_update(w_moe_in, grad_w_moe_in, mom_w_moe_in, avg_w_moe_in)
    new_w_moe_out, next_mom_w_moe_out, next_avg_w_moe_out, step_w_moe_out = apply_update(w_moe_out, grad_w_moe_out, mom_w_moe_out, avg_w_moe_out)
    new_w_shared_in, next_mom_w_shared_in, next_avg_w_shared_in, unused_shared_in = apply_update(w_shared_in, grad_w_shared_in, mom_w_shared_in, avg_w_shared_in)
    new_w_shared_out, next_mom_w_shared_out, next_avg_w_shared_out, unused_shared_out = apply_update(w_shared_out, grad_w_shared_out, mom_w_shared_out, avg_w_shared_out)
    return (output, grad_tokens, grad_norm_gains, new_norm_gains, next_mom_norm_gains, next_avg_norm_gains, grad_w_qkv, new_w_qkv, next_mom_w_qkv, next_avg_w_qkv, grad_w_out, new_w_out, next_mom_w_out, next_avg_w_out, grad_w_router, new_w_router, next_mom_w_router, next_avg_w_router, grad_w_moe_in, new_w_moe_in, next_mom_w_moe_in, next_avg_w_moe_in, grad_w_moe_out, step_w_moe_out, next_mom_w_moe_out, next_avg_w_moe_out, grad_w_shared_in, new_w_shared_in, next_mom_w_shared_in, next_avg_w_shared_in, grad_w_shared_out, new_w_shared_out, next_mom_w_shared_out, next_avg_w_shared_out)
```

```python
import jax
import jax.numpy as jnp
from jax import lax
from jax.sharding import PartitionSpec as P

QUERY_HEADS = 12
KEY_VALUE_HEADS = 4
HEAD_SIZE = 128
EXPERTS = 64
FE = 512
FS = 1024
CAP = 16


NORM_EPSILON = 1e-05
MASKED_SCORE = -1e30
LEARN_RATE = 0.001
MOMENTUM = 0.5
DECAY = 0.5


def silu_slope(values):
    sigmoid = jax.nn.sigmoid(values)
    return sigmoid * (1.0 + values * (1.0 - sigmoid))


def norm_forward(values, gain_row):
    inverse = lax.rsqrt(jnp.mean(values * values, axis=-1, keepdims=True) + NORM_EPSILON)
    return (values * inverse * gain_row, inverse)


def norm_backward(values, inverse, gain_row, upstream):
    scaled = gain_row * upstream
    gain_grad = jnp.sum(upstream * values * inverse, axis=0)
    input_grad = inverse * scaled - values * inverse**3 * jnp.mean(
        scaled * values, axis=-1, keepdims=True
    )
    return (input_grad, gain_grad)


def contract_rows(left_side, right_side):
    return lax.dot_general(
        left_side, right_side, (((0,), (0,)), ((), ())), preferred_element_type=jnp.float32
    )


def contract_cols(left_side, right_side):
    return lax.dot_general(
        left_side, right_side, (((1,), (1,)), ((), ())), preferred_element_type=jnp.float32
    )


def low(values):
    return values.astype(jnp.bfloat16)


def gather_rows(shard, axis):
    return lax.all_gather(shard, axis, axis=0, tiled=True)


def scatter_rows(partial, axis):
    return lax.psum_scatter(partial, axis, scatter_dimension=0, tiled=True)


def exchange(pieces, axis):
    return lax.all_to_all(pieces, axis, split_axis=0, concat_axis=0, tiled=True)


def visible_keys(doc_starts, key_index):
    group_rows = doc_starts.shape[0]
    own_index = lax.axis_index("blk")
    query_pos = own_index * group_rows + jnp.arange(group_rows, dtype=jnp.int32)
    key_pos = key_index * group_rows + jnp.arange(group_rows, dtype=jnp.int32)
    return (key_pos[None, :] <= query_pos[:, None]) & (key_pos[None, :] >= doc_starts[:, None])


def block_scores(queries, keys, visible):
    scores = jnp.einsum("rqd,kd->rqk", queries, keys, preferred_element_type=jnp.float32)
    return jnp.where(visible[None], scores * HEAD_SIZE ** (-0.5), MASKED_SCORE)


def key_block(pairs, key_index, group_rows):
    block = lax.dynamic_slice_in_dim(pairs, key_index * group_rows, group_rows, 0)
    return (block[:, :HEAD_SIZE], block[:, HEAD_SIZE:])


def attend_forward(queries, pairs, doc_starts):
    heads_per_group, group_rows, head_dim = queries.shape
    own_index = lax.axis_index("blk")

    def absorb(key_index, state):
        running, row_total, weighted = state
        keys, values = key_block(pairs, key_index, group_rows)
        scores = block_scores(queries, keys, visible_keys(doc_starts, key_index))
        new_max = jnp.maximum(running, jnp.max(scores, axis=-1, keepdims=True))
        weights = jnp.where(scores > 0.5 * MASKED_SCORE, jnp.exp(scores - new_max), 0.0)
        factor = jnp.exp(running - new_max)
        row_total = row_total * factor + jnp.sum(weights, axis=-1, keepdims=True)
        weighted = weighted * factor + jnp.einsum(
            "rqk,kd->rqd", low(weights), values, preferred_element_type=jnp.float32
        )
        return (new_max, row_total, weighted)

    state = (
        jnp.full((heads_per_group, group_rows, 1), MASKED_SCORE, jnp.float32),
        jnp.zeros((heads_per_group, group_rows, 1), jnp.float32),
        jnp.zeros((heads_per_group, group_rows, head_dim), jnp.float32),
    )
    first = doc_starts[0] // group_rows
    running, row_total, weighted = lax.fori_loop(first, own_index + 1, absorb, state)
    return (weighted / row_total, running + jnp.log(row_total))


def attend_backward(queries, pairs, grad_heads, attn_rows, log_total, doc_starts):
    heads_per_group, group_rows, head_dim = queries.shape
    own_index = lax.axis_index("blk")
    score_scale = HEAD_SIZE ** (-0.5)
    row_delta = jnp.sum(grad_heads.astype(jnp.float32) * attn_rows, axis=-1, keepdims=True)

    def absorb(key_index, grads):
        grad_queries, grad_pairs = grads
        keys, values = key_block(pairs, key_index, group_rows)
        scores = block_scores(queries, keys, visible_keys(doc_starts, key_index))
        weights = jnp.exp(scores - log_total)
        grad_weights = jnp.einsum(
            "rqd,kd->rqk", grad_heads, values, preferred_element_type=jnp.float32
        )
        grad_scores = low(weights * (grad_weights - row_delta))
        grad_queries = grad_queries + score_scale * jnp.einsum(
            "rqk,kd->rqd", grad_scores, keys, preferred_element_type=jnp.float32
        )
        key_part = score_scale * jnp.einsum(
            "rqk,rqd->kd", grad_scores, queries, preferred_element_type=jnp.float32
        )
        value_part = jnp.einsum(
            "rqk,rqd->kd", low(weights), grad_heads, preferred_element_type=jnp.float32
        )
        part = low(jnp.concatenate([key_part, value_part], axis=-1))
        grad_pairs = lax.dynamic_update_slice_in_dim(grad_pairs, part, key_index * group_rows, 0)
        return (grad_queries, grad_pairs)

    grads = (jnp.zeros(queries.shape, jnp.float32), jnp.zeros(pairs.shape, jnp.bfloat16))
    first = doc_starts[0] // group_rows
    return lax.fori_loop(first, own_index + 1, absorb, grads)


def apply_update(weight, gradient, moment, average):
    moment_new = MOMENTUM * moment + gradient
    change = -LEARN_RATE * (gradient + MOMENTUM * moment_new)
    weight_new = weight + change
    average_new = DECAY * average + (1.0 - DECAY) * weight_new
    return (gradient, weight_new, moment_new, average_new, change)


def local(
    tokens,
    cotangent,
    doc_starts,
    routes,
    expert_slots,
    norm_gains,
    qkv_projection_weight,
    w_out,
    w_router,
    w_moe_in,
    w_moe_out,
    w_shared_in,
    w_shared_out,
    mom_norm_gains,
    momentum_qkv_weight,
    mom_w_out,
    mom_w_router,
    mom_w_moe_in,
    mom_w_moe_out,
    mom_w_shared_in,
    mom_w_shared_out,
    avg_norm_gains,
    averaged_qkv_weight,
    avg_w_out,
    avg_w_router,
    avg_w_moe_in,
    avg_w_moe_out,
    avg_w_shared_in,
    avg_w_shared_out,
):
    rows, model_width = tokens.shape
    heads = lax.axis_size("head")
    blocks = lax.axis_size("blk")
    per_group = QUERY_HEADS // KEY_VALUE_HEADS
    query_width = per_group * HEAD_SIZE
    pair_width = 2 * HEAD_SIZE
    shared_width = FS // heads
    slice_width = model_width // heads
    local_experts = w_moe_in.shape[0]
    weight_rows = w_router.shape[0]
    group_rows = rows * heads
    cell_count = EXPERTS * CAP
    own_head = lax.axis_index("head")

    def split_heads(weight):
        return low(weight).reshape(weight_rows, heads, -1)

    def every_head(weight):
        return jnp.broadcast_to(low(weight)[:, None, :], (weight_rows, heads, weight.shape[1]))

    def spread(pieces):
        packed = jnp.concatenate(pieces, axis=-1).transpose(1, 0, 2)
        return gather_rows(exchange(packed, "head").reshape(heads * weight_rows, -1), "blk")

    def collect(partial):
        mine = scatter_rows(low(partial), "blk").reshape(heads, weight_rows, -1)
        return exchange(mine, "head").transpose(1, 0, 2).astype(jnp.float32)

    first_pack = spread([split_heads(qkv_projection_weight), every_head(norm_gains.T)])
    inverse_one = lax.rsqrt(jnp.mean(tokens * tokens, axis=-1, keepdims=True) + NORM_EPSILON)
    unit_one = gather_rows(low(tokens * inverse_one), "head")
    qkv_width = query_width + pair_width
    qkv_cols = first_pack[:, :qkv_width]
    gain_rows = first_pack[:, qkv_width:].astype(jnp.float32).T
    input_one = low(unit_one.astype(jnp.float32) * gain_rows[0])
    projected = low(jnp.dot(input_one, qkv_cols, preferred_element_type=jnp.float32))
    queries = projected[:, :query_width].reshape(group_rows, per_group, HEAD_SIZE)
    queries = queries.transpose(1, 0, 2)
    pairs = gather_rows(projected[:, query_width:], "blk")
    second_pack = spread(
        [
            split_heads(w_out.T),
            split_heads(w_shared_in[:, :FS]),
            split_heads(w_shared_in[:, FS:]),
            split_heads(w_shared_out.T),
            every_head(w_router),
        ]
    )
    out_cols = second_pack[:, :query_width]
    shared_in_cols = second_pack[:, query_width : query_width + 2 * shared_width]
    shared_out_cols = second_pack[:, query_width + 2 * shared_width :][:, :shared_width]
    router_full = second_pack[:, query_width + 3 * shared_width :]
    grad_low = low(cotangent)
    grad_low_all = gather_rows(grad_low, "head")
    moe_in_low = low(w_moe_in)
    moe_out_low = low(w_moe_out)

    attn_rows, log_total = attend_forward(queries, pairs, doc_starts)
    attn_flat = low(attn_rows).transpose(1, 0, 2).reshape(group_rows, query_width)
    mixed_rows = tokens + scatter_rows(low(contract_cols(attn_flat, out_cols)), "head").astype(
        jnp.float32
    )
    normed_two, inverse_two = norm_forward(mixed_rows, gain_rows[1])
    input_two = low(normed_two)
    input_two_all = gather_rows(input_two, "head")

    router_logits = jnp.dot(input_two, router_full, preferred_element_type=jnp.float32)
    route_match = routes[:, :, None] == jnp.arange(EXPERTS, dtype=jnp.int32)[None, None, :]
    gate_probs = jax.nn.softmax(
        jnp.sum(jnp.where(route_match, router_logits[:, None, :], 0.0), axis=-1), axis=-1
    )
    cell_codes = jnp.where(expert_slots >= 0, routes * CAP + expert_slots, -1)
    cell_match = cell_codes[:, :, None] == jnp.arange(cell_count, dtype=jnp.int32)[None, None, :]
    dispatch_table = low(jnp.any(cell_match, axis=1))
    combine_weights = low(jnp.sum(jnp.where(cell_match, gate_probs[:, :, None], 0.0), axis=1))

    def to_owners(table, values):
        cells = low(contract_rows(table, values))
        return cells.reshape(blocks, local_experts * CAP, heads, slice_width).transpose(0, 2, 1, 3)

    outgoing = jnp.concatenate(
        [to_owners(dispatch_table, input_two), to_owners(combine_weights, grad_low)], axis=-1
    ).reshape(blocks * heads, local_experts, CAP, 2 * slice_width)
    received = exchange(outgoing, ("blk", "head"))
    cells_in = received[..., :slice_width]
    grads_in = received[..., slice_width:]
    gate_up_part = jnp.einsum(
        "secf,efn->escn", cells_in, moe_in_low, preferred_element_type=jnp.float32
    )
    grad_hidden_part = jnp.einsum(
        "secf,ekf->esck", grads_in, moe_out_low, preferred_element_type=jnp.float32
    )
    expert_part = low(jnp.concatenate([gate_up_part, grad_hidden_part], axis=-1))
    expert_sum = scatter_rows(expert_part.reshape(-1, 3 * FE), "head").astype(jnp.float32)
    expert_gate = expert_sum[:, :FE]
    expert_up = expert_sum[:, FE : 2 * FE]
    grad_hidden = expert_sum[:, 2 * FE :]
    expert_acts = low(
        jnp.concatenate(
            [
                jax.nn.silu(expert_gate) * expert_up,
                grad_hidden * expert_up * silu_slope(expert_gate),
                grad_hidden * jax.nn.silu(expert_gate),
            ],
            axis=-1,
        )
    )
    acts_all = gather_rows(expert_acts, "head").reshape(
        local_experts, blocks * heads, CAP, 3 * FE
    )
    hidden_all = acts_all[..., :FE]
    grad_gate_up = acts_all[..., FE:]
    rows_part = jnp.einsum(
        "esck,ekf->secf", hidden_all, moe_out_low, preferred_element_type=jnp.float32
    )
    grad_cells_part = jnp.einsum(
        "escn,efn->secf", grad_gate_up, moe_in_low, preferred_element_type=jnp.float32
    )
    back = exchange(
        jnp.concatenate([low(rows_part), low(grad_cells_part)], axis=-1), ("blk", "head")
    )
    back = back.reshape(blocks, heads, local_experts * CAP, 2, slice_width)
    back = back.transpose(3, 0, 2, 1, 4).reshape(2, cell_count, model_width)
    returned = back[0]
    grad_returned = back[1]
    moe_in_grad = jnp.einsum(
        "secf,escn->efn", cells_in, grad_gate_up, preferred_element_type=jnp.float32
    )
    moe_out_grad = jnp.einsum(
        "esck,secf->ekf", hidden_all, grads_in, preferred_element_type=jnp.float32
    )

    shared_gate_up = jnp.dot(input_two_all, shared_in_cols, preferred_element_type=jnp.float32)
    shared_gate = shared_gate_up[:, :shared_width]
    shared_up = shared_gate_up[:, shared_width:]
    shared_hidden = low(jax.nn.silu(shared_gate) * shared_up)
    grad_shared_hidden = jnp.dot(grad_low_all, shared_out_cols, preferred_element_type=jnp.float32)
    grad_shared_gate_up = low(
        jnp.concatenate(
            [
                grad_shared_hidden * shared_up * silu_slope(shared_gate),
                grad_shared_hidden * jax.nn.silu(shared_gate),
            ],
            axis=-1,
        )
    )
    shared_part = jnp.concatenate(
        [
            low(contract_cols(shared_hidden, shared_out_cols)),
            low(contract_cols(grad_shared_gate_up, shared_in_cols)),
        ],
        axis=-1,
    )
    shared_sum = scatter_rows(shared_part, "head").astype(jnp.float32)

    expert_out = jnp.dot(combine_weights, returned, preferred_element_type=jnp.float32)
    output = mixed_rows + shared_sum[:, :model_width] + expert_out
    grad_combine = contract_cols(grad_low, returned)
    grad_gates = jnp.sum(jnp.where(cell_match, grad_combine[:, None, :], 0.0), axis=-1)
    grad_chosen = gate_probs * (
        grad_gates - jnp.sum(gate_probs * grad_gates, axis=-1, keepdims=True)
    )
    grad_logits = low(jnp.sum(jnp.where(route_match, grad_chosen[:, :, None], 0.0), axis=1))
    grad_input_two = (
        shared_sum[:, model_width:]
        + contract_cols(grad_logits, router_full)
        + jnp.dot(dispatch_table, grad_returned, preferred_element_type=jnp.float32)
    )
    grad_mixed_norm, grad_gain_two = norm_backward(
        mixed_rows, inverse_two, gain_rows[1], grad_input_two
    )
    grad_mixed = cotangent + grad_mixed_norm
    mixed_pack = gather_rows(jnp.concatenate([low(grad_mixed), grad_logits], axis=-1), "head")
    grad_mixed_all = mixed_pack[:, :model_width]
    grad_logits_own = lax.dynamic_slice_in_dim(
        mixed_pack[:, model_width:], own_head * (EXPERTS // heads), EXPERTS // heads, 1
    )
    second_grads = collect(
        jnp.concatenate(
            [
                contract_rows(grad_mixed_all, attn_flat),
                contract_rows(input_two_all, grad_shared_gate_up),
                contract_rows(grad_low_all, shared_hidden),
                contract_rows(input_two_all, grad_logits_own),
            ],
            axis=-1,
        )
    )

    def own_columns(grads, start, width):
        return grads[:, :, start : start + width].reshape(weight_rows, heads * width)

    out_part = own_columns(second_grads, 0, query_width).T
    shared_in_part = jnp.concatenate(
        [
            own_columns(second_grads, query_width, shared_width),
            own_columns(second_grads, query_width + shared_width, shared_width),
        ],
        axis=-1,
    )
    shared_out_part = own_columns(second_grads, query_width + 2 * shared_width, shared_width).T
    router_part = own_columns(second_grads, query_width + 3 * shared_width, EXPERTS // heads)

    grad_heads = low(jnp.dot(grad_mixed_all, out_cols, preferred_element_type=jnp.float32))
    grad_heads = grad_heads.reshape(group_rows, per_group, HEAD_SIZE).transpose(1, 0, 2)
    grad_queries, grad_pairs = attend_backward(
        queries, pairs, grad_heads, attn_rows, log_total, doc_starts
    )
    pair_parts = exchange(grad_pairs.reshape(blocks, group_rows, pair_width), "blk")
    grad_projected = jnp.concatenate(
        [
            low(grad_queries).transpose(1, 0, 2).reshape(group_rows, query_width),
            low(jnp.sum(pair_parts.astype(jnp.float32), axis=0)),
        ],
        axis=-1,
    )
    input_grad_part = contract_cols(grad_projected, qkv_cols)
    gain_one_part = jnp.sum(input_grad_part * unit_one.astype(jnp.float32), axis=0)
    gain_parts = jnp.stack([gain_one_part, grad_gain_two], axis=-1)
    first_grads = collect(
        jnp.concatenate([contract_rows(input_one, grad_projected), gain_parts], axis=-1)
    )
    qkv_part = own_columns(first_grads, 0, qkv_width)
    gain_part = jnp.sum(first_grads[:, :, qkv_width:], axis=1).T
    grad_input_one = scatter_rows(low(input_grad_part), "head").astype(jnp.float32)
    grad_token_norm, unused_gain = norm_backward(tokens, inverse_one, gain_rows[0], grad_input_one)
    grad_tokens = grad_mixed + grad_token_norm

    gains_new = apply_update(norm_gains, gain_part, mom_norm_gains, avg_norm_gains)
    qkv_new = apply_update(
        qkv_projection_weight, qkv_part, momentum_qkv_weight, averaged_qkv_weight
    )
    out_new = apply_update(w_out, out_part, mom_w_out, avg_w_out)
    router_new = apply_update(w_router, router_part, mom_w_router, avg_w_router)
    moe_in_new = apply_update(w_moe_in, moe_in_grad, mom_w_moe_in, avg_w_moe_in)
    moe_out_new = apply_update(w_moe_out, moe_out_grad, mom_w_moe_out, avg_w_moe_out)
    shared_in_new = apply_update(w_shared_in, shared_in_part, mom_w_shared_in, avg_w_shared_in)
    shared_out_new = apply_update(w_shared_out, shared_out_part, mom_w_shared_out, avg_w_shared_out)
    return (
        output,
        grad_tokens,
        gains_new[0],
        gains_new[1],
        gains_new[2],
        gains_new[3],
        qkv_new[0],
        qkv_new[1],
        qkv_new[2],
        qkv_new[3],
        out_new[0],
        out_new[1],
        out_new[2],
        out_new[3],
        router_new[0],
        router_new[1],
        router_new[2],
        router_new[3],
        moe_in_new[0],
        moe_in_new[1],
        moe_in_new[2],
        moe_in_new[3],
        moe_out_new[0],
        moe_out_new[4],
        moe_out_new[2],
        moe_out_new[3],
        shared_in_new[0],
        shared_in_new[1],
        shared_in_new[2],
        shared_in_new[3],
        shared_out_new[0],
        shared_out_new[1],
        shared_out_new[2],
        shared_out_new[3],
    )


def solution(mesh):
    in_specs = (
        P(("blk", "head"), None),
        P(("blk", "head"), None),
        P("blk"),
        P(("blk", "head"), None),
        P(("blk", "head"), None),
        P(None, ("blk", "head")),
        P(("blk", "head"), None),
        P(None, ("blk", "head")),
        P(("blk", "head"), None),
        P("blk", "head", None),
        P("blk", None, "head"),
        P(("blk", "head"), None),
        P(None, ("blk", "head")),
        P(None, ("blk", "head")),
        P(("blk", "head"), None),
        P(None, ("blk", "head")),
        P(("blk", "head"), None),
        P("blk", "head", None),
        P("blk", None, "head"),
        P(("blk", "head"), None),
        P(None, ("blk", "head")),
        P(None, ("blk", "head")),
        P(("blk", "head"), None),
        P(None, ("blk", "head")),
        P(("blk", "head"), None),
        P("blk", "head", None),
        P("blk", None, "head"),
        P(("blk", "head"), None),
        P(None, ("blk", "head")),
    )
    out_specs = (
        P(("blk", "head"), None),
        P(("blk", "head"), None),
        P(None, ("blk", "head")),
        P(None, ("blk", "head")),
        P(None, ("blk", "head")),
        P(None, ("blk", "head")),
        P(("blk", "head"), None),
        P(("blk", "head"), None),
        P(("blk", "head"), None),
        P(("blk", "head"), None),
        P(None, ("blk", "head")),
        P(None, ("blk", "head")),
        P(None, ("blk", "head")),
        P(None, ("blk", "head")),
        P(("blk", "head"), None),
        P(("blk", "head"), None),
        P(("blk", "head"), None),
        P(("blk", "head"), None),
        P("blk", "head", None),
        P("blk", "head", None),
        P("blk", "head", None),
        P("blk", "head", None),
        P("blk", None, "head"),
        P("blk", None, "head"),
        P("blk", None, "head"),
        P("blk", None, "head"),
        P(("blk", "head"), None),
        P(("blk", "head"), None),
        P(("blk", "head"), None),
        P(("blk", "head"), None),
        P(None, ("blk", "head")),
        P(None, ("blk", "head")),
        P(None, ("blk", "head")),
        P(None, ("blk", "head")),
    )
    return jax.shard_map(local, mesh=mesh, in_specs=in_specs, out_specs=out_specs, check_vma=False)
```
